32 devices in a mesh: energy: 4 (over y, x), space: 8 (over z, core).
Axes of the slice: x: 2, y: 2, z: 4, core: 2. Of those that a mesh axis runs over, the one named last changes fastest.
Arguments:
- right_side: float32 [4, 64, 64, 512], P(None, 'space', None, 'energy')
- rate: float32 [64, 64, 512], P('space', None, 'energy'), may hold values from 0.5 to 2
- fields: float32 [2, 64, 64], P(None, 'space'), may hold values from -3 to 3
- speed: float32 [512], P('energy'), may hold values from 0.3 to 1
- regions: int32 [64, 64], P('space'), may hold values from 0 to 3
- contacts: int32 [64, 64], P('space'), may hold values 0 or 1
- offsets: int32 [4], replicated, may hold values from 12 to 24, as said below
- phonon: float32 [4, 2], replicated, may hold values from 0.1 to 0.6
Outputs:
- state: float32 [4, 64, 64, 512], P(None, 'space', None, 'energy')
- norms: float32 [2, 4], replicated
The draws below stay inside these ranges and needn't reach their ends.
Inputs may be any that keep to these rules, and one draw needn't show every extreme that they name: `offsets`: each region's phonon energy lies between 12 and 24 bins; some region has exactly 24.
All inputs are finite; a program needn't handle non-finite values. No bound on the sum of `contacts` on one device may be relied on, other than what follows from the above.
Results may differ from the reference program's by a relative error of at most 0.0001.
Values sent between devices are 32-bit elements; how exact they have to be, the bound alone decides.
A program may use at most 64 MiB of HBM per device.

```python
import math
import jax
import jax.numpy as jnp
from jax import lax

COEFS = 4
Y = 64
HOP = 24
REGIONS = 4
SWEEPS = 2
X = 64
E = 512


def draw_right_side(key, part):
    xs = jnp.arange(X, dtype=jnp.float32) / max(X - 1, 1)
    es = jnp.arange(E, dtype=jnp.float32) / max(E - 1, 1)
    profile = (1.0 + 2.0 * xs)[:, None, None] * (1.0 + 2.0 * es)[None, None, :]
    base = jax.random.normal(jax.random.fold_in(key, 1), (COEFS, X, Y, E), dtype=jnp.float32)
    return (base * profile[None]).astype(jnp.float32)


def draw_offsets(key, part):
    values = jax.random.randint(jax.random.fold_in(key, 5), (REGIONS,), HOP // 2, HOP + 1)
    where_top = jax.random.randint(jax.random.fold_in(key, 6), (), 0, REGIONS)
    return jnp.where(jnp.arange(REGIONS) == where_top, HOP, values).astype(jnp.int32)


def touch_ends(entries, rng, smallest, top_value):
    dims = entries.shape
    place = [jax.random.randint(jax.random.fold_in(rng, axis), (), 0, dims[axis]) for axis in range(len(dims))]
    entries = entries.at[tuple(place)].set(smallest)
    longest = dims.index(max(dims))
    place[longest] = (place[longest] + 1) % dims[longest]
    return entries.at[tuple(place)].set(top_value)


def shard_levels(rng, extent, cuts, smallest, high):
    level = 1.0
    for axis_at, parts in cuts:
        heights = jax.random.uniform(jax.random.fold_in(jax.random.fold_in(rng, 6), axis_at), (parts,), jnp.float32, smallest / len(cuts), high / len(cuts))
        level = level * jnp.repeat(jnp.exp(heights), extent[axis_at] // parts).reshape((-1,) + (1,) * (len(extent) - 1 - axis_at))
    return level


def centred(key, dims, scale, limit, pieces=(), held_as=jnp.bfloat16):
    result = scale * jax.random.normal(key, dims, jnp.float32)
    if pieces:
        result = result * shard_levels(key, dims, pieces, -0.22, 0.18)
    return jnp.clip(result, -limit, limit).astype(held_as)


def setup_inputs(seed: int = 0) -> dict:
    key_of = jax.random.split(jax.random.key(seed), 9)
    right_side = draw_right_side(jax.random.fold_in(key_of[8], 71), 0)
    rate = jnp.clip(jnp.exp(math.log(2.0) - 1.3862944 * jax.random.uniform(key_of[1], (X, Y, E), jnp.float32) ** shard_levels(key_of[1], (X, Y, E), ((0, 8), (2, 4)), -0.2, 0.2)), 0.5, 2.0)
    fields = centred(key_of[2], (2, X, Y), 0.5, 3.0, ((1, 8),), jnp.float32)
    speed = jnp.clip(jnp.exp(math.log(1.0) - 1.2039728 * jax.random.uniform(key_of[3], (E,), jnp.float32) ** shard_levels(key_of[3], (E,), ((0, 4),), -0.2, 0.2)), 0.3, 1.0)
    regions = touch_ends(jax.random.randint(key_of[4], (X, Y), 0, REGIONS), jax.random.fold_in(key_of[4], 1), 0, REGIONS - 1).astype(jnp.int32)
    contacts = touch_ends((jax.random.randint(key_of[5], (X, Y), 0, 8) < 1).astype(jnp.int32), jax.random.fold_in(key_of[5], 1), 0, 1)
    offsets = draw_offsets(jax.random.fold_in(key_of[8], 71), 0)
    phonon = jnp.clip(jnp.exp(jax.random.uniform(key_of[7], (REGIONS, 2), jnp.float32, math.log(0.1), math.log(0.6))), 0.1, 0.6)
    return {"right_side": right_side, "rate": rate, "fields": fields, "speed": speed, "regions": regions, "contacts": contacts, "offsets": offsets, "phonon": phonon}


diffusion = 0.25

def operator_of(field, diagonal, push_x, push_y, speed, regions, offsets, phonon):
    padded_x = jnp.pad(field, ((0, 0), (1, 1), (0, 0), (0, 0)))
    after_x = padded_x[:, 2:]
    before_x = padded_x[:, :-2]
    padded_y = jnp.pad(field, ((0, 0), (0, 0), (1, 1), (0, 0)))
    after_y = padded_y[:, :, 2:]
    before_y = padded_y[:, :, :-2]
    beside = after_x + before_x + after_y + before_y
    velocity = speed[None, None, :]
    drift_zero = 0.5 * velocity * (after_x[1] - before_x[1] + (after_y[2] - before_y[2]))
    drift_one = 0.5 * velocity * (after_x[0] - before_x[0])
    drift_two = 0.5 * velocity * (after_y[0] - before_y[0])
    width = field.shape[3]
    padded_e = jnp.pad(field[0], ((0, 0), (0, 0), (HOP, HOP)))
    scatter = jnp.zeros_like(field[0])
    for region in range(REGIONS):
        below = lax.dynamic_slice_in_dim(padded_e, (HOP - offsets[region]).astype(jnp.int32), width, 2)
        above = lax.dynamic_slice_in_dim(padded_e, (HOP + offsets[region]).astype(jnp.int32), width, 2)
        inside = (regions == region).astype(field.dtype)[:, :, None]
        scatter = scatter + inside * (phonon[region, 0] * below + phonon[region, 1] * above)
    out_zero = diagonal * field[0] + push_x * field[1] + push_y * field[2] - diffusion * beside[0] + drift_zero - scatter
    out_one = -push_x * field[0] + diagonal * field[1] - diffusion * beside[1] + drift_one
    out_two = -push_y * field[0] + diagonal * field[2] - diffusion * beside[2] + drift_two
    out_three = diagonal * field[3] - diffusion * beside[3]
    return jnp.stack([out_zero, out_one, out_two, out_three])

def block_solve(resid, diagonal, push_x, push_y):
    first = (diagonal * resid[0] - push_x * resid[1] - push_y * resid[2]) / (diagonal * diagonal + push_x * push_x + push_y * push_y)
    second = (resid[1] + push_x * first) / diagonal
    third = (resid[2] + push_y * first) / diagonal
    fourth = resid[3] / diagonal
    return jnp.stack([first, second, third, fourth])

def reference(right_side, rate, fields, speed, regions, contacts, offsets, phonon):
    diagonal = rate + 4.0 * diffusion
    push_x = fields[0][:, :, None]
    push_y = fields[1][:, :, None]
    pinned = (contacts == 1)[None, :, :, None]
    state = jnp.zeros_like(right_side)
    resid = right_side
    norm_rows = []
    for sweep in range(SWEEPS):
        solved = block_solve(resid, diagonal, push_x, push_y)
        state = state + jnp.where(pinned, resid, solved)
        image = operator_of(state, diagonal, push_x, push_y, speed, regions, offsets, phonon)
        resid = jnp.where(pinned, right_side - state, right_side - image)
        norm_rows.append(jnp.sqrt(lax.optimization_barrier(jnp.sum(resid * resid, axis=(1, 2, 3)))))
    return (state, jnp.stack(norm_rows))
```

```python
import functools

import jax
import jax.numpy as jnp
from jax import lax
from jax.experimental import pallas as pl
from jax.experimental.pallas import tpu as pltpu
from jax.sharding import PartitionSpec as P

HOP = 24
REGIONS = 4
SWEEPS = 2
COEFS = 4
PAD = 8
ROWS = 16

diffusion = 0.25

MESH = pl.DeviceIdType.MESH


def kernel(
    n_energy,
    n_space,
    offsets_ref,
    phonon_ref,
    right_hbm,
    rate_hbm,
    fields_ref,
    speed_ref,
    regions_ref,
    contacts_ref,
    state_hbm,
    norms_ref,
    right,
    rate,
    field,
    cell_x,
    cell_y,
    cell_pin,
    cell_off,
    cell_absorb,
    cell_emit,
    inv_diag,
    inv_det,
    pack_low,
    pack_high,
    from_low,
    from_high,
    sums,
    in_sem,
    out_sem,
    x_send,
    x_recv,
    e_send,
    e_recv,
    n_send,
    n_recv,
):
    nx, ny, width = right.shape[1:]
    lanes_each = 1
    while lanes_each < HOP:
        lanes_each *= 2
    groups = width // lanes_each
    e = lax.axis_index("energy")
    s = lax.axis_index("space")
    total = n_energy * n_space
    me = e * n_space + s

    barrier = pltpu.get_barrier_semaphore()

    def greet(step, carry):
        other = lax.rem(me + step, total)
        pl.semaphore_signal(
            barrier,
            inc=1,
            device_id=(other // n_space, lax.rem(other, n_space)),
            device_id_type=MESH,
        )
        return carry

    lax.fori_loop(1, total, greet, 0)

    load_right = pltpu.make_async_copy(right_hbm, right, in_sem.at[0])
    load_rate = pltpu.make_async_copy(rate_hbm, rate, in_sem.at[1])
    load_right.start()
    load_rate.start()

    region = regions_ref[...]
    off = jnp.zeros_like(region)
    absorb = jnp.zeros(region.shape, jnp.float32)
    emit = jnp.zeros(region.shape, jnp.float32)
    for r in range(REGIONS):
        inside = region == r
        off = jnp.where(inside, offsets_ref[r], off)
        absorb = jnp.where(inside, phonon_ref[r, 0], absorb)
        emit = jnp.where(inside, phonon_ref[r, 1], emit)
    for source, target in (
        (fields_ref[0], cell_x),
        (fields_ref[1], cell_y),
        (contacts_ref[...], cell_pin),
        (off, cell_off),
        (absorb, cell_absorb),
        (emit, cell_emit),
    ):
        turned = source.T
        for x in range(nx):
            target[x] = jnp.broadcast_to(turned[:, x : x + 1], (ny, width))

    zero_rows = jnp.zeros((PAD, width), jnp.float32)
    for k in range(SWEEPS):
        for c in range(COEFS):
            for x in range(1, nx + 1):
                field[k, c, x, 0:PAD] = zero_rows
                field[k, c, x, PAD + ny : 2 * PAD + ny] = zero_rows

    zero_plane = jnp.zeros((ny, width), jnp.float32)

    @pl.when(s == 0)
    def _():
        for k in range(SWEEPS):
            for c in range(COEFS):
                field[k, c, 0, PAD : PAD + ny] = zero_plane

    @pl.when(s == n_space - 1)
    def _():
        for k in range(SWEEPS):
            for c in range(COEFS):
                field[k, c, nx + 1, PAD : PAD + ny] = zero_plane

    @pl.when(e == 0)
    def _():
        for k in range(SWEEPS):
            for q in range(from_low.shape[1]):
                from_low[k, q] = zero_plane

    @pl.when(e == n_energy - 1)
    def _():
        for k in range(SWEEPS):
            for q in range(from_high.shape[1]):
                from_high[k, q] = zero_plane

    load_rate.wait()
    load_right.wait()

    def solve(r, px, py, diag, inv_d, inv_t):
        first = (diag * r[0] - px * r[1] - py * r[2]) * inv_t
        return (
            first,
            (r[1] + px * first) * inv_d,
            (r[2] + py * first) * inv_d,
            r[3] * inv_d,
        )

    def first_state(x, carry):
        for y in range(0, ny, ROWS):
            rows = pl.ds(y, ROWS)
            diag = rate[x, rows] + 4.0 * diffusion
            px, py = cell_x[x, rows], cell_y[x, rows]
            inv_d = 1.0 / diag
            inv_t = 1.0 / (diag * diag + px * px + py * py)
            inv_diag[x, rows] = inv_d
            inv_det[x, rows] = inv_t
            r = [right[c, x, rows] for c in range(COEFS)]
            u = solve(r, px, py, diag, inv_d, inv_t)
            pinned = cell_pin[x, rows] == 1
            for c in range(COEFS):
                field[0, c, x + 1, pl.ds(PAD + y, ROWS)] = jnp.where(pinned, r[c], u[c])
        return carry

    lax.fori_loop(0, nx, first_state, 0)
    pl.semaphore_wait(barrier, total - 1)

    plane_group = lax.broadcasted_iota(jnp.int32, (ny, width), 1) // lanes_each
    inner = pl.ds(PAD, ny)

    def to_right(k):
        return pltpu.make_async_remote_copy(
            src_ref=field.at[k, :, nx, inner],
            dst_ref=field.at[k, :, 0, inner],
            send_sem=x_send.at[k, 0],
            recv_sem=x_recv.at[k, 0],
            device_id=(e, s + 1),
            device_id_type=MESH,
        )

    def to_left(k):
        return pltpu.make_async_remote_copy(
            src_ref=field.at[k, :, 1, inner],
            dst_ref=field.at[k, :, nx + 1, inner],
            send_sem=x_send.at[k, 1],
            recv_sem=x_recv.at[k, 1],
            device_id=(e, s - 1),
            device_id_type=MESH,
        )

    def to_upper(k):
        return pltpu.make_async_remote_copy(
            src_ref=pack_high.at[k],
            dst_ref=from_low.at[k],
            send_sem=e_send.at[k, 0],
            recv_sem=e_recv.at[k, 0],
            device_id=(e + 1, s),
            device_id_type=MESH,
        )

    def to_lower(k):
        return pltpu.make_async_remote_copy(
            src_ref=pack_low.at[k],
            dst_ref=from_high.at[k],
            send_sem=e_send.at[k, 1],
            recv_sem=e_recv.at[k, 1],
            device_id=(e - 1, s),
            device_id_type=MESH,
        )

    has_right, has_left = s < n_space - 1, s > 0
    has_upper, has_lower = e < n_energy - 1, e > 0

    def exchange(k):
        @pl.when(has_right)
        def _():
            to_right(k).start()

        @pl.when(has_left)
        def _():
            to_left(k).start()

        for q in range(pack_low.shape[1]):
            low = zero_plane
            high = zero_plane
            for j in range(groups):
                x = q * groups + j
                if x >= nx:
                    break
                plane = field[k, 0, x + 1, inner]
                here = plane_group == j
                turn_low = lanes_each * j
                turn_high = (lanes_each * (j + 1)) % width
                rolled_low = pltpu.roll(plane, turn_low, 1) if turn_low else plane
                rolled_high = pltpu.roll(plane, turn_high, 1) if turn_high else plane
                low = jnp.where(here, rolled_low, low)
                high = jnp.where(here, rolled_high, high)
            pack_low[k, q] = low
            pack_high[k, q] = high

        @pl.when(has_upper)
        def _():
            to_upper(k).start()

        @pl.when(has_lower)
        def _():
            to_lower(k).start()

    def arrive(k):
        @pl.when(has_lower)
        def _():
            to_upper(k).wait_recv()

        @pl.when(has_upper)
        def _():
            to_lower(k).wait_recv()

        @pl.when(has_left)
        def _():
            to_right(k).wait_recv()

        @pl.when(has_right)
        def _():
            to_left(k).wait_recv()

    lane = lax.broadcasted_iota(jnp.int32, (ROWS, width), 1)
    velocity = jnp.broadcast_to(0.5 * speed_ref[...], (ROWS, width))

    def residual(k, x, y, j, q):
        rows = pl.ds(y, ROWS)
        mid = pl.ds(PAD + y, ROWS)
        f = [field[k, c, x + 1, mid] for c in range(COEFS)]
        xp = [field[k, c, x + 2, mid] for c in range(COEFS)]
        xm = [field[k, c, x, mid] for c in range(COEFS)]
        yp = [field[k, c, x + 1, pl.ds(PAD + y + 1, ROWS)] for c in range(COEFS)]
        ym = [field[k, c, x + 1, pl.ds(PAD + y - 1, ROWS)] for c in range(COEFS)]
        diag = rate[x, rows] + 4.0 * diffusion
        px, py = cell_x[x, rows], cell_y[x, rows]
        nb = [xp[c] + xm[c] + (yp[c] + ym[c]) for c in range(COEFS)]
        back_low = (lanes_each * (groups - 1 - j)) % width
        back_high = (width - lanes_each * j) % width
        low = from_low[k, q, rows]
        high = from_high[k, q, rows]
        low = pltpu.roll(low, back_low, 1) if back_low else low
        high = pltpu.roll(high, back_high, 1) if back_high else high
        beyond = jnp.where(lane < width // 2, high, low)
        off = cell_off[x, rows]
        below = jnp.take_along_axis(
            jnp.where(lane < width - off, f[0], beyond),
            lax.rem(lane - off + width, width),
            axis=1,
            mode="promise_in_bounds",
        )
        above = jnp.take_along_axis(
            jnp.where(lane < off, beyond, f[0]),
            lax.rem(lane + off, width),
            axis=1,
            mode="promise_in_bounds",
        )
        scatter = cell_absorb[x, rows] * below + cell_emit[x, rows] * above
        image = [
            diag * f[0]
            + px * f[1]
            + py * f[2]
            - diffusion * nb[0]
            + velocity * (xp[1] - xm[1] + (yp[2] - ym[2]))
            - scatter,
            diag * f[1] - px * f[0] - diffusion * nb[1] + velocity * (xp[0] - xm[0]),
            diag * f[2] - py * f[0] - diffusion * nb[2] + velocity * (yp[0] - ym[0]),
            diag * f[3] - diffusion * nb[3],
        ]
        pinned = cell_pin[x, rows] == 1
        resid = [
            right[c, x, rows] - jnp.where(pinned, f[c], image[c]) for c in range(COEFS)
        ]
        return f, resid, pinned, px, py, diag

    def folded(value):
        square = value * value
        out = square[0:8]
        for i in range(8, ROWS, 8):
            out = out + square[i : i + 8]
        return out

    def sweep(k, last):
        def planes(q, carry):
            acc = list(carry)
            for j in range(groups):
                x = q * groups + j
                for y in range(0, ny, ROWS):
                    f, resid, pinned, px, py, diag = residual(k, x, y, j, q)
                    for c in range(COEFS):
                        acc[c] = acc[c] + folded(resid[c])
                    if not last:
                        rows = pl.ds(y, ROWS)
                        u = solve(resid, px, py, diag, inv_diag[x, rows], inv_det[x, rows])
                        for c in range(COEFS):
                            field[k + 1, c, x + 1, pl.ds(PAD + y, ROWS)] = f[c] + jnp.where(
                                pinned, resid[c], u[c]
                            )
            return tuple(acc)

        start = tuple(jnp.zeros((8, width), jnp.float32) for _ in range(COEFS))
        return lax.fori_loop(0, nx // groups, planes, start)

    partial = []
    store = pltpu.make_async_copy(
        field.at[SWEEPS - 1, :, pl.ds(1, nx), inner], state_hbm, out_sem
    )
    for k in range(SWEEPS):
        exchange(k)
        if k == SWEEPS - 1:
            store.start()
        arrive(k)
        partial.extend(sweep(k, k == SWEEPS - 1))

    spot = lax.broadcasted_iota(jnp.int32, (1, width), 1)
    mine = jnp.zeros((1, width), jnp.float32)
    for i, value in enumerate(partial):
        whole = jnp.sum(jnp.sum(value, axis=0, keepdims=True), axis=1, keepdims=True)
        mine = jnp.where(spot == i, whole, mine)
    sums[me] = mine

    def tell(step):
        other = lax.rem(me + step, total)
        return pltpu.make_async_remote_copy(
            src_ref=sums.at[me],
            dst_ref=sums.at[me],
            send_sem=n_send.at[other],
            recv_sem=n_recv.at[me],
            device_id=(other // n_space, lax.rem(other, n_space)),
            device_id_type=MESH,
        )

    def heard(step):
        other = lax.rem(me + step, total)
        return pltpu.make_async_remote_copy(
            src_ref=sums.at[other],
            dst_ref=sums.at[other],
            send_sem=n_send.at[other],
            recv_sem=n_recv.at[other],
            device_id=(other // n_space, lax.rem(other, n_space)),
            device_id_type=MESH,
        )

    def tell_start(step, carry):
        tell(step).start()
        return carry

    lax.fori_loop(1, total, tell_start, 0)
    for k in range(SWEEPS):

        @pl.when(has_right)
        def _():
            to_right(k).wait_send()

        @pl.when(has_left)
        def _():
            to_left(k).wait_send()

        @pl.when(has_upper)
        def _():
            to_upper(k).wait_send()

        @pl.when(has_lower)
        def _():
            to_lower(k).wait_send()

    store.wait()

    def heard_wait(step, carry):
        heard(step).wait_recv()
        return carry

    lax.fori_loop(1, total, heard_wait, 0)

    def tell_wait(step, carry):
        tell(step).wait_send()
        return carry

    lax.fori_loop(1, total, tell_wait, 0)
    norm = jnp.sqrt(jnp.sum(sums[...], axis=0))
    norm = jnp.broadcast_to(norm, (8, width))
    for k in range(SWEEPS):
        turned = pltpu.roll(norm, width - COEFS * k, 1) if k else norm
        norms_ref[k : k + 1, :] = turned[0:1, 0:COEFS]


def solution(mesh):
    n_energy, n_space = mesh.shape["energy"], mesh.shape["space"]

    def local(right_side, rate, fields, speed, regions, contacts, offsets, phonon):
        coefs, nx, ny, width = right_side.shape
        lanes_each = 1
        while lanes_each < HOP:
            lanes_each *= 2
        packs = -(-nx // (width // lanes_each))
        plane = (nx, ny, width)
        vmem = pl.BlockSpec(memory_space=pltpu.VMEM)
        smem = pl.BlockSpec(memory_space=pltpu.SMEM)
        hbm = pl.BlockSpec(memory_space=pl.ANY)
        f32 = jnp.float32
        pack = pltpu.VMEM((SWEEPS, packs, ny, width), f32)
        return pl.pallas_call(
            functools.partial(kernel, n_energy, n_space),
            out_shape=(
                jax.ShapeDtypeStruct(right_side.shape, f32),
                jax.ShapeDtypeStruct((SWEEPS, coefs), f32),
            ),
            in_specs=[smem, smem, hbm, hbm, vmem, vmem, vmem, vmem],
            out_specs=(hbm, vmem),
            scratch_shapes=[
                pltpu.VMEM(right_side.shape, f32),
                pltpu.VMEM(plane, f32),
                pltpu.VMEM((SWEEPS, coefs, nx + 2, ny + 2 * PAD, width), f32),
                pltpu.VMEM(plane, f32),
                pltpu.VMEM(plane, f32),
                pltpu.VMEM(plane, jnp.int32),
                pltpu.VMEM(plane, jnp.int32),
                pltpu.VMEM(plane, f32),
                pltpu.VMEM(plane, f32),
                pltpu.VMEM(plane, f32),
                pltpu.VMEM(plane, f32),
                pack,
                pack,
                pack,
                pack,
                pltpu.VMEM((n_energy * n_space, 1, width), f32),
                pltpu.SemaphoreType.DMA((2,)),
                pltpu.SemaphoreType.DMA,
                pltpu.SemaphoreType.DMA((SWEEPS, 2)),
                pltpu.SemaphoreType.DMA((SWEEPS, 2)),
                pltpu.SemaphoreType.DMA((SWEEPS, 2)),
                pltpu.SemaphoreType.DMA((SWEEPS, 2)),
                pltpu.SemaphoreType.DMA((n_energy * n_space,)),
                pltpu.SemaphoreType.DMA((n_energy * n_space,)),
            ],
            compiler_params=pltpu.CompilerParams(collective_id=0, has_side_effects=True),
        )(offsets, phonon, right_side, rate, fields, speed.reshape(1, width), regions, contacts)

    in_specs = (
        P(None, "space", None, "energy"),
        P("space", None, "energy"),
        P(None, "space", None),
        P("energy"),
        P("space", None),
        P("space", None),
        P(),
        P(),
    )
    out_specs = (P(None, "space", None, "energy"), P())
    return jax.shard_map(local, mesh=mesh, in_specs=in_specs, out_specs=out_specs, check_vma=False)
```

```python
import functools

import jax
import jax.numpy as jnp
from jax import lax
from jax.experimental import pallas as pl
from jax.experimental.pallas import tpu as pltpu
from jax.sharding import PartitionSpec as P

HOP = 24
REGIONS = 4
SWEEPS = 2
COEFS = 4
PAD = 8
ROWS = 16

diffusion = 0.25

MESH = pl.DeviceIdType.MESH


def kernel(
    n_energy,
    n_space,
    offsets_hbm,
    phonon_hbm,
    right_hbm,
    rate_hbm,
    fields_hbm,
    speed_hbm,
    regions_hbm,
    contacts_hbm,
    state_ref,
    sums_ref,
    offsets_ref,
    phonon_ref,
    fields_ref,
    speed_ref,
    regions_ref,
    contacts_ref,
    right,
    rate,
    field,
    cell_x,
    cell_y,
    cell_pin,
    cell_off,
    cell_absorb,
    cell_emit,
    inv_diag,
    inv_det,
    pack_low,
    pack_high,
    from_low,
    from_high,
    beyond,
    along_energy,
    along_space,
    in_sem,
    out_sem,
    x_send,
    x_recv,
    e_send,
    e_recv,
    n_send,
    n_recv,
    m_send,
    m_recv,
):
    nx, ny, width = right.shape[1:]
    groups = width // HOP
    e = lax.axis_index("energy")
    s = lax.axis_index("space")

    barrier = pltpu.get_barrier_semaphore()
    for step in range(1, n_energy):
        pl.semaphore_signal(
            barrier,
            inc=1,
            device_id=(lax.rem(e + step, n_energy), s),
            device_id_type=MESH,
        )
    for step in range(1, n_space):
        pl.semaphore_signal(
            barrier,
            inc=1,
            device_id=(e, lax.rem(s + step, n_space)),
            device_id_type=MESH,
        )

    loads = [
        pltpu.make_async_copy(source, target, in_sem.at[i])
        for i, (source, target) in enumerate(
            (
                (offsets_hbm, offsets_ref),
                (phonon_hbm, phonon_ref),
                (fields_hbm, fields_ref),
                (speed_hbm, speed_ref),
                (regions_hbm, regions_ref),
                (contacts_hbm, contacts_ref),
                (rate_hbm, rate),
                (right_hbm, right),
            )
        )
    ]
    for load in loads:
        load.start()

    zero_rows = jnp.zeros((PAD, width), jnp.float32)
    for k in range(SWEEPS):
        for c in range(COEFS):
            for x in range(1, nx + 1):
                field[k, c, x, 0:PAD] = zero_rows
                field[k, c, x, PAD + ny : 2 * PAD + ny] = zero_rows

    zero_plane = jnp.zeros((ny, width), jnp.float32)

    @pl.when(s == 0)
    def _():
        for k in range(SWEEPS):
            for c in range(COEFS):
                field[k, c, 0, PAD : PAD + ny] = zero_plane

    @pl.when(s == n_space - 1)
    def _():
        for k in range(SWEEPS):
            for c in range(COEFS):
                field[k, c, nx + 1, PAD : PAD + ny] = zero_plane

    @pl.when(e == 0)
    def _():
        for k in range(SWEEPS):
            from_low[k] = jnp.zeros(from_low.shape[1:], jnp.float32)

    @pl.when(e == n_energy - 1)
    def _():
        for k in range(SWEEPS):
            from_high[k] = jnp.zeros(from_high.shape[1:], jnp.float32)

    for load in loads[:-2]:
        load.wait()

    region = regions_ref[...]
    off = jnp.zeros_like(region)
    absorb = jnp.zeros(region.shape, jnp.float32)
    emit = jnp.zeros(region.shape, jnp.float32)
    for r in range(REGIONS):
        inside = region == r
        off = jnp.where(inside, offsets_ref[r], off)
        absorb = jnp.where(inside, phonon_ref[0, r], absorb)
        emit = jnp.where(inside, phonon_ref[1, r], emit)
    for source, target in (
        (fields_ref[0], cell_x),
        (fields_ref[1], cell_y),
        (contacts_ref[...], cell_pin),
        (off, cell_off),
        (absorb, cell_absorb),
        (emit, cell_emit),
    ):
        turned = source.T
        for x in range(nx):
            target[x] = jnp.broadcast_to(turned[:, x : x + 1], (ny, width))

    for load in loads[-2:]:
        load.wait()

    def solve(r, px, py, diag, inv_d, inv_t):
        first = (diag * r[0] - px * r[1] - py * r[2]) * inv_t
        return (
            first,
            (r[1] + px * first) * inv_d,
            (r[2] + py * first) * inv_d,
            r[3] * inv_d,
        )

    def first_state(x, carry):
        for y in range(0, ny, ROWS):
            rows = pl.ds(y, ROWS)
            diag = rate[x, rows] + 4.0 * diffusion
            px, py = cell_x[x, rows], cell_y[x, rows]
            inv_d = 1.0 / diag
            inv_t = 1.0 / (diag * diag + px * px + py * py)
            inv_diag[x, rows] = inv_d
            inv_det[x, rows] = inv_t
            r = [right[c, x, rows] for c in range(COEFS)]
            u = solve(r, px, py, diag, inv_d, inv_t)
            pinned = cell_pin[x, rows] == 1
            for c in range(COEFS):
                field[0, c, x + 1, pl.ds(PAD + y, ROWS)] = jnp.where(pinned, r[c], u[c])
        return carry

    lax.fori_loop(0, nx, first_state, 0)
    pl.semaphore_wait(barrier, n_energy + n_space - 2)

    unit_lane = lax.broadcasted_iota(jnp.int32, (8, width), 1)
    units = [(x, y) for x in range(nx) for y in range(0, ny, 8)]
    inner = pl.ds(PAD, ny)

    def to_right(k):
        return pltpu.make_async_remote_copy(
            src_ref=field.at[k, :, nx, inner],
            dst_ref=field.at[k, :, 0, inner],
            send_sem=x_send.at[k, 0],
            recv_sem=x_recv.at[k, 0],
            device_id=(e, s + 1),
            device_id_type=MESH,
        )

    def to_left(k):
        return pltpu.make_async_remote_copy(
            src_ref=field.at[k, :, 1, inner],
            dst_ref=field.at[k, :, nx + 1, inner],
            send_sem=x_send.at[k, 1],
            recv_sem=x_recv.at[k, 1],
            device_id=(e, s - 1),
            device_id_type=MESH,
        )

    def to_upper(k):
        return pltpu.make_async_remote_copy(
            src_ref=pack_high.at[k],
            dst_ref=from_low.at[k],
            send_sem=e_send.at[k, 0],
            recv_sem=e_recv.at[k, 0],
            device_id=(e + 1, s),
            device_id_type=MESH,
        )

    def to_lower(k):
        return pltpu.make_async_remote_copy(
            src_ref=pack_low.at[k],
            dst_ref=from_high.at[k],
            send_sem=e_send.at[k, 1],
            recv_sem=e_recv.at[k, 1],
            device_id=(e - 1, s),
            device_id_type=MESH,
        )

    has_right, has_left = s < n_space - 1, s > 0
    has_upper, has_lower = e < n_energy - 1, e > 0

    def turn(value, by):
        by = by % width
        return pltpu.roll(value, by, 1) if by else value

    def exchange(k):
        @pl.when(has_right)
        def _():
            to_right(k).start()

        @pl.when(has_left)
        def _():
            to_left(k).start()

        for q in range(pack_low.shape[1]):
            low = jnp.zeros((8, width), jnp.float32)
            high = jnp.zeros((8, width), jnp.float32)
            for j, (x, y) in enumerate(units[q * groups : (q + 1) * groups]):
                part = field[k, 0, x + 1, pl.ds(PAD + y, 8)]
                here = (unit_lane >= HOP * j) & (unit_lane < HOP * (j + 1))
                low = jnp.where(here, turn(part, HOP * j), low)
                high = jnp.where(here, turn(part, HOP * (j + 1)), high)
            pack_low[k, q] = low
            pack_high[k, q] = high

        @pl.when(has_upper)
        def _():
            to_upper(k).start()

        @pl.when(has_lower)
        def _():
            to_lower(k).start()

    def arrive(k):
        @pl.when(has_lower)
        def _():
            to_upper(k).wait_recv()

        @pl.when(has_upper)
        def _():
            to_lower(k).wait_recv()

        @pl.when(has_left)
        def _():
            to_right(k).wait_recv()

        @pl.when(has_right)
        def _():
            to_left(k).wait_recv()

        for i, (x, y) in enumerate(units):
            q, j = i // groups, i % groups
            beyond[x, pl.ds(y, 8)] = jnp.where(
                unit_lane < width // 2,
                turn(from_high[k, q], -HOP * j),
                turn(from_low[k, q], -HOP * (j + 1)),
            )

    lane = lax.broadcasted_iota(jnp.int32, (ROWS, width), 1)
    velocity = jnp.broadcast_to(0.5 * speed_ref[...], (ROWS, width))

    def residual(k, x, y):
        rows = pl.ds(y, ROWS)
        mid = pl.ds(PAD + y, ROWS)
        f = [field[k, c, x + 1, mid] for c in range(COEFS)]
        xp = [field[k, c, x + 2, mid] for c in range(COEFS)]
        xm = [field[k, c, x, mid] for c in range(COEFS)]
        yp = [field[k, c, x + 1, pl.ds(PAD + y + 1, ROWS)] for c in range(COEFS)]
        ym = [field[k, c, x + 1, pl.ds(PAD + y - 1, ROWS)] for c in range(COEFS)]
        diag = rate[x, rows] + 4.0 * diffusion
        px, py = cell_x[x, rows], cell_y[x, rows]
        nb = [xp[c] + xm[c] + (yp[c] + ym[c]) for c in range(COEFS)]
        outside = beyond[x, rows]
        off = cell_off[x, rows]
        below = jnp.take_along_axis(
            jnp.where(lane < width - off, f[0], outside),
            lax.rem(lane - off + width, width),
            axis=1,
            mode="promise_in_bounds",
        )
        above = jnp.take_along_axis(
            jnp.where(lane < off, outside, f[0]),
            lax.rem(lane + off, width),
            axis=1,
            mode="promise_in_bounds",
        )
        scatter = cell_absorb[x, rows] * below + cell_emit[x, rows] * above
        image = [
            diag * f[0]
            + px * f[1]
            + py * f[2]
            - diffusion * nb[0]
            + velocity * (xp[1] - xm[1] + (yp[2] - ym[2]))
            - scatter,
            diag * f[1] - px * f[0] - diffusion * nb[1] + velocity * (xp[0] - xm[0]),
            diag * f[2] - py * f[0] - diffusion * nb[2] + velocity * (yp[0] - ym[0]),
            diag * f[3] - diffusion * nb[3],
        ]
        pinned = cell_pin[x, rows] == 1
        resid = [
            right[c, x, rows] - jnp.where(pinned, f[c], image[c]) for c in range(COEFS)
        ]
        return f, resid, pinned, px, py, diag

    def folded(value):
        square = value * value
        out = square[0:8]
        for i in range(8, ROWS, 8):
            out = out + square[i : i + 8]
        return out

    def sweep(k, last):
        def plane(x, carry):
            acc = list(carry)
            for y in range(0, ny, ROWS):
                f, resid, pinned, px, py, diag = residual(k, x, y)
                for c in range(COEFS):
                    acc[c] = acc[c] + folded(resid[c])
                if not last:
                    rows = pl.ds(y, ROWS)
                    u = solve(resid, px, py, diag, inv_diag[x, rows], inv_det[x, rows])
                    for c in range(COEFS):
                        field[k + 1, c, x + 1, pl.ds(PAD + y, ROWS)] = f[c] + jnp.where(
                            pinned, resid[c], u[c]
                        )
            return tuple(acc)

        start = tuple(jnp.zeros((8, width), jnp.float32) for _ in range(COEFS))
        return lax.fori_loop(0, nx, plane, start)

    partial = []
    store = pltpu.make_async_copy(
        field.at[SWEEPS - 1, :, pl.ds(1, nx), inner], state_ref, out_sem
    )
    for k in range(SWEEPS):
        exchange(k)
        if k == SWEEPS - 1:
            store.start()
        arrive(k)
        partial.extend(sweep(k, k == SWEEPS - 1))

    spot = lax.broadcasted_iota(jnp.int32, (1, width), 1)
    mine = jnp.zeros((1, width), jnp.float32)
    for i, value in enumerate(partial):
        whole = jnp.sum(jnp.sum(value, axis=0, keepdims=True), axis=1, keepdims=True)
        mine = jnp.where(spot == i, whole, mine)
    along_energy[e] = mine

    def tell(sums, size, place, to, sems, step):
        return pltpu.make_async_remote_copy(
            src_ref=sums.at[place],
            dst_ref=sums.at[place],
            send_sem=sems[0].at[step],
            recv_sem=sems[1].at[place],
            device_id=to(lax.rem(place + step, size)),
            device_id_type=MESH,
        )

    def heard(sums, size, place, to, sems, step):
        other = lax.rem(place + step, size)
        return pltpu.make_async_remote_copy(
            src_ref=sums.at[other],
            dst_ref=sums.at[other],
            send_sem=sems[0].at[step],
            recv_sem=sems[1].at[other],
            device_id=to(other),
            device_id_type=MESH,
        )

    first = (along_energy, n_energy, e, lambda i: (i, s), (n_send, n_recv))
    second = (along_space, n_space, s, lambda i: (e, i), (m_send, m_recv))
    for step in range(1, n_energy):
        tell(*first, step).start()
    for step in range(1, n_energy):
        heard(*first, step).wait_recv()
    along_space[s] = jnp.sum(along_energy[...], axis=0)
    for step in range(1, n_space):
        tell(*second, step).start()
    for k in range(SWEEPS):

        @pl.when(has_right)
        def _():
            to_right(k).wait_send()

        @pl.when(has_left)
        def _():
            to_left(k).wait_send()

        @pl.when(has_upper)
        def _():
            to_upper(k).wait_send()

        @pl.when(has_lower)
        def _():
            to_lower(k).wait_send()

    for step in range(1, n_energy):
        tell(*first, step).wait_send()
    store.wait()
    for step in range(1, n_space):
        heard(*second, step).wait_recv()
    for step in range(1, n_space):
        tell(*second, step).wait_send()
    sums_ref[...] = jnp.sum(along_space[...], axis=0)


def finish(state, sums_ref, state_hbm, norms_ref, sem):
    store = pltpu.make_async_copy(state, state_hbm, sem)
    store.start()
    width = sums_ref.shape[1]
    norm = jnp.broadcast_to(jnp.sqrt(sums_ref[...]), (8, width))
    for k in range(SWEEPS):
        turned = pltpu.roll(norm, width - COEFS * k, 1) if k else norm
        norms_ref[k : k + 1, :] = turned[0:1, 0:COEFS]
    store.wait()


def solution(mesh):
    n_energy, n_space = mesh.shape["energy"], mesh.shape["space"]

    def local(right_side, rate, fields, speed, regions, contacts, offsets, phonon):
        coefs, nx, ny, width = right_side.shape
        packs = -(-(nx * ny // 8) // (width // HOP))
        plane = (nx, ny, width)
        vmem = pl.BlockSpec(memory_space=pltpu.VMEM)
        hbm = pl.BlockSpec(memory_space=pl.ANY)
        f32 = jnp.float32
        pack = pltpu.VMEM((SWEEPS, packs, 8, width), f32)
        state, sums = pl.pallas_call(
            functools.partial(kernel, n_energy, n_space),
            out_shape=(
                pltpu.VMEM(right_side.shape, f32),
                pltpu.VMEM((1, width), f32),
            ),
            in_specs=[pl.BlockSpec(memory_space=pltpu.HBM)] * 8,
            out_specs=(vmem, vmem),
            scratch_shapes=[
                pltpu.SMEM(offsets.shape, offsets.dtype),
                pltpu.SMEM((phonon.shape[1], phonon.shape[0]), f32),
                pltpu.VMEM(fields.shape, f32),
                pltpu.VMEM((1, width), f32),
                pltpu.VMEM(regions.shape, regions.dtype),
                pltpu.VMEM(contacts.shape, contacts.dtype),
                pltpu.VMEM(right_side.shape, f32),
                pltpu.VMEM(plane, f32),
                pltpu.VMEM((SWEEPS, coefs, nx + 2, ny + 2 * PAD, width), f32),
                pltpu.VMEM(plane, f32),
                pltpu.VMEM(plane, f32),
                pltpu.VMEM(plane, jnp.int32),
                pltpu.VMEM(plane, jnp.int32),
                pltpu.VMEM(plane, f32),
                pltpu.VMEM(plane, f32),
                pltpu.VMEM(plane, f32),
                pltpu.VMEM(plane, f32),
                pack,
                pack,
                pack,
                pack,
                pltpu.VMEM(plane, f32),
                pltpu.VMEM((n_energy, 1, width), f32),
                pltpu.VMEM((n_space, 1, width), f32),
                pltpu.SemaphoreType.DMA((8,)),
                pltpu.SemaphoreType.DMA,
                pltpu.SemaphoreType.DMA((SWEEPS, 2)),
                pltpu.SemaphoreType.DMA((SWEEPS, 2)),
                pltpu.SemaphoreType.DMA((SWEEPS, 2)),
                pltpu.SemaphoreType.DMA((SWEEPS, 2)),
                pltpu.SemaphoreType.DMA((n_energy,)),
                pltpu.SemaphoreType.DMA((n_energy,)),
                pltpu.SemaphoreType.DMA((n_space,)),
                pltpu.SemaphoreType.DMA((n_space,)),
            ],
            compiler_params=pltpu.CompilerParams(
                collective_id=0, has_side_effects=True, vmem_limit_bytes=24 << 20
            ),
        )(
            *(
                pltpu.with_memory_space_constraint(value, pltpu.HBM)
                for value in (
                    offsets,
                    phonon.T,
                    right_side,
                    rate,
                    fields,
                    speed.reshape(1, width),
                    regions,
                    contacts,
                )
            )
        )
        return pl.pallas_call(
            finish,
            out_shape=(
                jax.ShapeDtypeStruct(right_side.shape, f32),
                jax.ShapeDtypeStruct((SWEEPS, coefs), f32),
            ),
            in_specs=[vmem, vmem],
            out_specs=(hbm, vmem),
            scratch_shapes=[pltpu.SemaphoreType.DMA],
            compiler_params=pltpu.CompilerParams(vmem_limit_bytes=8 << 20),
        )(state, sums)

    in_specs = (
        P(None, "space", None, "energy"),
        P("space", None, "energy"),
        P(None, "space", None),
        P("energy"),
        P("space", None),
        P("space", None),
        P(),
        P(),
    )
    out_specs = (P(None, "space", None, "energy"), P())
    return jax.shard_map(local, mesh=mesh, in_specs=in_specs, out_specs=out_specs, check_vma=False)
```

```python
import functools

import jax
import jax.numpy as jnp
from jax import lax
from jax.experimental import pallas as pl
from jax.experimental.pallas import tpu as pltpu
from jax.sharding import PartitionSpec as P

HOP = 24
REGIONS = 4
SWEEPS = 2
COEFS = 4
PAD = 8
ROWS = 16

diffusion = 0.25

MESH = pl.DeviceIdType.MESH


def kernel(
    n_energy,
    n_space,
    offsets_hbm,
    phonon_hbm,
    right_hbm,
    rate_hbm,
    fields_hbm,
    speed_hbm,
    regions_hbm,
    contacts_hbm,
    state_ref,
    sums_ref,
    offsets_ref,
    phonon_ref,
    fields_ref,
    speed_ref,
    regions_ref,
    contacts_ref,
    right,
    rate,
    field,
    cell_x,
    cell_y,
    cell_pin,
    cell_off,
    cell_absorb,
    cell_emit,
    inv_diag,
    inv_det,
    pack_low,
    pack_high,
    from_low,
    from_high,
    beyond,
    along_energy,
    along_space,
    in_sem,
    out_sem,
    x_send,
    x_recv,
    e_send,
    e_recv,
    n_send,
    n_recv,
    m_send,
    m_recv,
):
    nx, ny, width = right.shape[1:]
    groups = width // HOP
    e = lax.axis_index("energy")
    s = lax.axis_index("space")

    barrier = pltpu.get_barrier_semaphore()
    for step in range(1, n_energy):
        pl.semaphore_signal(
            barrier,
            inc=1,
            device_id=(lax.rem(e + step, n_energy), s),
            device_id_type=MESH,
        )
    for step in range(1, n_space):
        pl.semaphore_signal(
            barrier,
            inc=1,
            device_id=(e, lax.rem(s + step, n_space)),
            device_id_type=MESH,
        )

    loads = [
        pltpu.make_async_copy(source, target, in_sem.at[i])
        for i, (source, target) in enumerate(
            (
                (offsets_hbm, offsets_ref),
                (phonon_hbm, phonon_ref),
                (fields_hbm, fields_ref),
                (speed_hbm, speed_ref),
                (regions_hbm, regions_ref),
                (contacts_hbm, contacts_ref),
                (rate_hbm, rate),
                *((right_hbm.at[c], right.at[c]) for c in range(COEFS)),
            )
        )
    ]
    for load in loads:
        load.start()

    zero_rows = jnp.zeros((PAD, width), jnp.float32)
    for k in range(SWEEPS):
        for c in range(COEFS):
            for x in range(1, nx + 1):
                field[k, c, x, 0:PAD] = zero_rows
                field[k, c, x, PAD + ny : 2 * PAD + ny] = zero_rows

    zero_plane = jnp.zeros((ny, width), jnp.float32)

    @pl.when(s == 0)
    def _():
        for k in range(SWEEPS):
            for c in range(COEFS):
                field[k, c, 0, PAD : PAD + ny] = zero_plane

    @pl.when(s == n_space - 1)
    def _():
        for k in range(SWEEPS):
            for c in range(COEFS):
                field[k, c, nx + 1, PAD : PAD + ny] = zero_plane

    @pl.when(e == 0)
    def _():
        for k in range(SWEEPS):
            from_low[k] = jnp.zeros(from_low.shape[1:], jnp.float32)

    @pl.when(e == n_energy - 1)
    def _():
        for k in range(SWEEPS):
            from_high[k] = jnp.zeros(from_high.shape[1:], jnp.float32)

    for load in loads[:6]:
        load.wait()

    region = regions_ref[...]
    off = jnp.zeros_like(region)
    absorb = jnp.zeros(region.shape, jnp.float32)
    emit = jnp.zeros(region.shape, jnp.float32)
    for r in range(REGIONS):
        inside = region == r
        off = jnp.where(inside, offsets_ref[r], off)
        absorb = jnp.where(inside, phonon_ref[0, r], absorb)
        emit = jnp.where(inside, phonon_ref[1, r], emit)
    for source, target in (
        (fields_ref[0], cell_x),
        (fields_ref[1], cell_y),
        (contacts_ref[...], cell_pin),
        (off, cell_off),
        (absorb, cell_absorb),
        (emit, cell_emit),
    ):
        turned = source.T
        for x in range(nx):
            target[x] = jnp.broadcast_to(turned[:, x : x + 1], (ny, width))

    for load in loads[6:]:
        load.wait()

    def solve(r, px, py, diag, inv_d, inv_t):
        first = (diag * r[0] - px * r[1] - py * r[2]) * inv_t
        return (
            first,
            (r[1] + px * first) * inv_d,
            (r[2] + py * first) * inv_d,
            r[3] * inv_d,
        )

    half = nx // 2

    def plane_at(i):
        turned, step = i % 2, i // 2
        return step + turned * (nx - 1 - 2 * step)

    def first_state(i, carry):
        x = plane_at(i)
        for y in range(0, ny, ROWS):
            rows = pl.ds(y, ROWS)
            diag = rate[x, rows] + 4.0 * diffusion
            px, py = cell_x[x, rows], cell_y[x, rows]
            inv_d = 1.0 / diag
            inv_t = 1.0 / (diag * diag + px * px + py * py)
            inv_diag[x, rows] = inv_d
            inv_det[x, rows] = inv_t
            r = [right[c, x, rows] for c in range(COEFS)]
            u = solve(r, px, py, diag, inv_d, inv_t)
            pinned = cell_pin[x, rows] == 1
            for c in range(COEFS):
                field[0, c, x + 1, pl.ds(PAD + y, ROWS)] = jnp.where(pinned, r[c], u[c])
        return carry

    lax.fori_loop(0, half, first_state, 0)
    pl.semaphore_wait(barrier, n_energy + n_space - 2)

    unit_lane = lax.broadcasted_iota(jnp.int32, (8, width), 1)
    units = [
        [(plane_at(i), y) for i in part for y in range(0, ny, 8)]
        for part in (range(half), range(half, nx))
    ]
    inner = pl.ds(PAD, ny)

    def to_right(k):
        return pltpu.make_async_remote_copy(
            src_ref=field.at[k, :, nx, inner],
            dst_ref=field.at[k, :, 0, inner],
            send_sem=x_send.at[k, 0],
            recv_sem=x_recv.at[k, 0],
            device_id=(e, s + 1),
            device_id_type=MESH,
        )

    def to_left(k):
        return pltpu.make_async_remote_copy(
            src_ref=field.at[k, :, 1, inner],
            dst_ref=field.at[k, :, nx + 1, inner],
            send_sem=x_send.at[k, 1],
            recv_sem=x_recv.at[k, 1],
            device_id=(e, s - 1),
            device_id_type=MESH,
        )

    def to_upper(k, g):
        return pltpu.make_async_remote_copy(
            src_ref=pack_high.at[k, g],
            dst_ref=from_low.at[k, g],
            send_sem=e_send.at[k, g, 0],
            recv_sem=e_recv.at[k, g, 0],
            device_id=(e + 1, s),
            device_id_type=MESH,
        )

    def to_lower(k, g):
        return pltpu.make_async_remote_copy(
            src_ref=pack_low.at[k, g],
            dst_ref=from_high.at[k, g],
            send_sem=e_send.at[k, g, 1],
            recv_sem=e_recv.at[k, g, 1],
            device_id=(e - 1, s),
            device_id_type=MESH,
        )

    has_right, has_left = s < n_space - 1, s > 0
    has_upper, has_lower = e < n_energy - 1, e > 0

    def turn(value, by):
        by = by % width
        return pltpu.roll(value, by, 1) if by else value

    def exchange(k, g):
        if g == 0:

            @pl.when(has_right)
            def _():
                to_right(k).start()

            @pl.when(has_left)
            def _():
                to_left(k).start()

        for q in range(pack_low.shape[2]):
            low = jnp.zeros((8, width), jnp.float32)
            high = jnp.zeros((8, width), jnp.float32)
            for j, (x, y) in enumerate(units[g][q * groups : (q + 1) * groups]):
                part = field[k, 0, x + 1, pl.ds(PAD + y, 8)]
                here = (unit_lane >= HOP * j) & (unit_lane < HOP * (j + 1))
                low = jnp.where(here, turn(part, HOP * j), low)
                high = jnp.where(here, turn(part, HOP * (j + 1)), high)
            pack_low[k, g, q] = low
            pack_high[k, g, q] = high

        @pl.when(has_upper)
        def _():
            to_upper(k, g).start()

        @pl.when(has_lower)
        def _():
            to_lower(k, g).start()

    def arrive(k, g):
        @pl.when(has_lower)
        def _():
            to_upper(k, g).wait_recv()

        @pl.when(has_upper)
        def _():
            to_lower(k, g).wait_recv()

        for i, (x, y) in enumerate(units[g]):
            q, j = i // groups, i % groups
            beyond[x, pl.ds(y, 8)] = jnp.where(
                unit_lane < width // 2,
                turn(from_high[k, g, q], -HOP * j),
                turn(from_low[k, g, q], -HOP * (j + 1)),
            )

        if g == 0:

            @pl.when(has_left)
            def _():
                to_right(k).wait_recv()

            @pl.when(has_right)
            def _():
                to_left(k).wait_recv()

    exchange(0, 0)
    lax.fori_loop(half, nx, first_state, 0)
    exchange(0, 1)

    lane = lax.broadcasted_iota(jnp.int32, (ROWS, width), 1)
    velocity = jnp.broadcast_to(0.5 * speed_ref[...], (ROWS, width))

    def residual(k, x, y):
        rows = pl.ds(y, ROWS)
        mid = pl.ds(PAD + y, ROWS)
        f = [field[k, c, x + 1, mid] for c in range(COEFS)]
        xp = [field[k, c, x + 2, mid] for c in range(COEFS)]
        xm = [field[k, c, x, mid] for c in range(COEFS)]
        yp = [field[k, c, x + 1, pl.ds(PAD + y + 1, ROWS)] for c in range(COEFS)]
        ym = [field[k, c, x + 1, pl.ds(PAD + y - 1, ROWS)] for c in range(COEFS)]
        diag = rate[x, rows] + 4.0 * diffusion
        px, py = cell_x[x, rows], cell_y[x, rows]
        nb = [xp[c] + xm[c] + (yp[c] + ym[c]) for c in range(COEFS)]
        outside = beyond[x, rows]
        off = cell_off[x, rows]
        below = jnp.take_along_axis(
            jnp.where(lane < width - off, f[0], outside),
            jnp.where(lane < off, lane - off + width, lane - off),
            axis=1,
            mode="promise_in_bounds",
        )
        above = jnp.take_along_axis(
            jnp.where(lane < off, outside, f[0]),
            jnp.where(lane < width - off, lane + off, lane + off - width),
            axis=1,
            mode="promise_in_bounds",
        )
        scatter = cell_absorb[x, rows] * below + cell_emit[x, rows] * above
        image = [
            diag * f[0]
            + px * f[1]
            + py * f[2]
            - diffusion * nb[0]
            + velocity * (xp[1] - xm[1] + (yp[2] - ym[2]))
            - scatter,
            diag * f[1] - px * f[0] - diffusion * nb[1] + velocity * (xp[0] - xm[0]),
            diag * f[2] - py * f[0] - diffusion * nb[2] + velocity * (yp[0] - ym[0]),
            diag * f[3] - diffusion * nb[3],
        ]
        pinned = cell_pin[x, rows] == 1
        resid = [
            right[c, x, rows] - jnp.where(pinned, f[c], image[c]) for c in range(COEFS)
        ]
        return f, resid, pinned, px, py, diag

    def folded(value):
        square = value * value
        out = square[0:8]
        for i in range(8, ROWS, 8):
            out = out + square[i : i + 8]
        return out

    def sweep(k, g, start):
        last = k == SWEEPS - 1

        def plane(i, carry):
            x = plane_at(i)
            acc = list(carry)
            for y in range(0, ny, ROWS):
                f, resid, pinned, px, py, diag = residual(k, x, y)
                for c in range(COEFS):
                    acc[c] = acc[c] + folded(resid[c])
                if not last:
                    rows = pl.ds(y, ROWS)
                    u = solve(resid, px, py, diag, inv_diag[x, rows], inv_det[x, rows])
                    for c in range(COEFS):
                        field[k + 1, c, x + 1, pl.ds(PAD + y, ROWS)] = f[c] + jnp.where(
                            pinned, resid[c], u[c]
                        )
            return tuple(acc)

        return lax.fori_loop(g * half, half if g == 0 else nx, plane, start)

    partial = []
    store = pltpu.make_async_copy(
        field.at[SWEEPS - 1, :, pl.ds(1, nx), inner], state_ref, out_sem
    )
    for k in range(SWEEPS):
        if k == SWEEPS - 1:
            store.start()
        acc = tuple(jnp.zeros((8, width), jnp.float32) for _ in range(COEFS))
        for g in range(2):
            arrive(k, g)
            acc = sweep(k, g, acc)
            if k < SWEEPS - 1:
                exchange(k + 1, g)
        partial.extend(acc)

    spot = lax.broadcasted_iota(jnp.int32, (1, width), 1)
    mine = jnp.zeros((1, width), jnp.float32)
    for i, value in enumerate(partial):
        whole = jnp.sum(jnp.sum(value, axis=0, keepdims=True), axis=1, keepdims=True)
        mine = jnp.where(spot == i, whole, mine)
    along_energy[e] = mine

    def tell(sums, size, place, to, sems, step):
        return pltpu.make_async_remote_copy(
            src_ref=sums.at[place],
            dst_ref=sums.at[place],
            send_sem=sems[0].at[step],
            recv_sem=sems[1].at[place],
            device_id=to(lax.rem(place + step, size)),
            device_id_type=MESH,
        )

    def heard(sums, size, place, to, sems, step):
        other = lax.rem(place + step, size)
        return pltpu.make_async_remote_copy(
            src_ref=sums.at[other],
            dst_ref=sums.at[other],
            send_sem=sems[0].at[step],
            recv_sem=sems[1].at[other],
            device_id=to(other),
            device_id_type=MESH,
        )

    first = (along_energy, n_energy, e, lambda i: (i, s), (n_send, n_recv))
    second = (along_space, n_space, s, lambda i: (e, i), (m_send, m_recv))
    for step in range(1, n_energy):
        tell(*first, step).start()
    for step in range(1, n_energy):
        heard(*first, step).wait_recv()
    along_space[s] = jnp.sum(along_energy[...], axis=0)
    for step in range(1, n_space):
        tell(*second, step).start()
    for k in range(SWEEPS):

        @pl.when(has_right)
        def _():
            to_right(k).wait_send()

        @pl.when(has_left)
        def _():
            to_left(k).wait_send()

        for g in range(2):

            @pl.when(has_upper)
            def _():
                to_upper(k, g).wait_send()

            @pl.when(has_lower)
            def _():
                to_lower(k, g).wait_send()

    for step in range(1, n_energy):
        tell(*first, step).wait_send()
    store.wait()
    for step in range(1, n_space):
        heard(*second, step).wait_recv()
    for step in range(1, n_space):
        tell(*second, step).wait_send()
    sums_ref[...] = jnp.sum(along_space[...], axis=0)


def finish(state, sums_ref, state_hbm, norms_ref, sem):
    stores = [
        pltpu.make_async_copy(state.at[c], state_hbm.at[c], sem.at[c]) for c in range(COEFS)
    ]
    for store in stores:
        store.start()
    width = sums_ref.shape[1]
    norm = jnp.broadcast_to(jnp.sqrt(sums_ref[...]), (8, width))
    for k in range(SWEEPS):
        turned = pltpu.roll(norm, width - COEFS * k, 1) if k else norm
        norms_ref[k : k + 1, :] = turned[0:1, 0:COEFS]
    for store in stores:
        store.wait()


def solution(mesh):
    n_energy, n_space = mesh.shape["energy"], mesh.shape["space"]

    def local(right_side, rate, fields, speed, regions, contacts, offsets, phonon):
        coefs, nx, ny, width = right_side.shape
        packs = -(-((nx - nx // 2) * ny // 8) // (width // HOP))
        plane = (nx, ny, width)
        vmem = pl.BlockSpec(memory_space=pltpu.VMEM)
        hbm = pl.BlockSpec(memory_space=pl.ANY)
        f32 = jnp.float32
        pack = pltpu.VMEM((SWEEPS, 2, packs, 8, width), f32)
        state, sums = pl.pallas_call(
            functools.partial(kernel, n_energy, n_space),
            out_shape=(
                pltpu.VMEM(right_side.shape, f32),
                pltpu.VMEM((1, width), f32),
            ),
            in_specs=[pl.BlockSpec(memory_space=pltpu.HBM)] * 8,
            out_specs=(vmem, vmem),
            scratch_shapes=[
                pltpu.SMEM(offsets.shape, offsets.dtype),
                pltpu.SMEM((phonon.shape[1], phonon.shape[0]), f32),
                pltpu.VMEM(fields.shape, f32),
                pltpu.VMEM((1, width), f32),
                pltpu.VMEM(regions.shape, regions.dtype),
                pltpu.VMEM(contacts.shape, contacts.dtype),
                pltpu.VMEM(right_side.shape, f32),
                pltpu.VMEM(plane, f32),
                pltpu.VMEM((SWEEPS, coefs, nx + 2, ny + 2 * PAD, width), f32),
                pltpu.VMEM(plane, f32),
                pltpu.VMEM(plane, f32),
                pltpu.VMEM(plane, jnp.int32),
                pltpu.VMEM(plane, jnp.int32),
                pltpu.VMEM(plane, f32),
                pltpu.VMEM(plane, f32),
                pltpu.VMEM(plane, f32),
                pltpu.VMEM(plane, f32),
                pack,
                pack,
                pack,
                pack,
                pltpu.VMEM(plane, f32),
                pltpu.VMEM((n_energy, 1, width), f32),
                pltpu.VMEM((n_space, 1, width), f32),
                pltpu.SemaphoreType.DMA((7 + coefs,)),
                pltpu.SemaphoreType.DMA,
                pltpu.SemaphoreType.DMA((SWEEPS, 2)),
                pltpu.SemaphoreType.DMA((SWEEPS, 2)),
                pltpu.SemaphoreType.DMA((SWEEPS, 2, 2)),
                pltpu.SemaphoreType.DMA((SWEEPS, 2, 2)),
                pltpu.SemaphoreType.DMA((n_energy,)),
                pltpu.SemaphoreType.DMA((n_energy,)),
                pltpu.SemaphoreType.DMA((n_space,)),
                pltpu.SemaphoreType.DMA((n_space,)),
            ],
            compiler_params=pltpu.CompilerParams(
                collective_id=0, has_side_effects=True, vmem_limit_bytes=24 << 20
            ),
        )(
            *(
                pltpu.with_memory_space_constraint(value, pltpu.HBM)
                for value in (
                    offsets,
                    phonon.T,
                    right_side,
                    rate,
                    fields,
                    speed.reshape(1, width),
                    regions,
                    contacts,
                )
            )
        )
        return pl.pallas_call(
            finish,
            out_shape=(
                jax.ShapeDtypeStruct(right_side.shape, f32),
                jax.ShapeDtypeStruct((SWEEPS, coefs), f32),
            ),
            in_specs=[vmem, vmem],
            out_specs=(hbm, vmem),
            scratch_shapes=[pltpu.SemaphoreType.DMA((coefs,))],
            compiler_params=pltpu.CompilerParams(vmem_limit_bytes=8 << 20),
        )(state, sums)

    in_specs = (
        P(None, "space", None, "energy"),
        P("space", None, "energy"),
        P(None, "space", None),
        P("energy"),
        P("space", None),
        P("space", None),
        P(),
        P(),
    )
    out_specs = (P(None, "space", None, "energy"), P())
    return jax.shard_map(local, mesh=mesh, in_specs=in_specs, out_specs=out_specs, check_vma=False)
```

```python
import functools

import jax
import jax.numpy as jnp
from jax import lax
from jax.experimental import pallas as pl
from jax.experimental.pallas import tpu as pltpu
from jax.sharding import PartitionSpec as P

HOP = 24
REGIONS = 4
SWEEPS = 2
COEFS = 4
PAD = 8
ROWS = 16

diffusion = 0.25

MESH = pl.DeviceIdType.MESH


def kernel(
    n_energy,
    n_space,
    offsets_hbm,
    phonon_hbm,
    right_hbm,
    rate_hbm,
    fields_hbm,
    speed_hbm,
    regions_hbm,
    contacts_hbm,
    state_ref,
    sums_ref,
    offsets_ref,
    phonon_ref,
    fields_ref,
    speed_ref,
    regions_ref,
    contacts_ref,
    right,
    rate,
    field,
    cell_x,
    cell_y,
    cell_pin,
    cell_off,
    cell_absorb,
    cell_emit,
    inv_diag,
    inv_det,
    pack_low,
    pack_high,
    from_low,
    from_high,
    beyond,
    sums,
    in_sem,
    out_sem,
    x_send,
    x_recv,
    e_send,
    e_recv,
    n_send,
    n_recv,
    known,
):
    nx, ny, width = right.shape[1:]
    groups = width // HOP
    e = lax.axis_index("energy")
    s = lax.axis_index("space")
    me = e * n_space + s

    barrier = pltpu.get_barrier_semaphore()
    for step in range(1, n_energy):
        pl.semaphore_signal(
            barrier,
            inc=1,
            device_id=(lax.rem(e + step, n_energy), s),
            device_id_type=MESH,
        )
    for step in range(1, n_space):
        pl.semaphore_signal(
            barrier,
            inc=1,
            device_id=(e, lax.rem(s + step, n_space)),
            device_id_type=MESH,
        )

    loads = [
        pltpu.make_async_copy(source, target, in_sem.at[i])
        for i, (source, target) in enumerate(
            (
                (offsets_hbm, offsets_ref),
                (phonon_hbm, phonon_ref),
                (fields_hbm, fields_ref),
                (speed_hbm, speed_ref),
                (regions_hbm, regions_ref),
                (contacts_hbm, contacts_ref),
                (rate_hbm, rate),
                *((right_hbm.at[c], right.at[c]) for c in range(COEFS)),
            )
        )
    ]
    for load in loads:
        load.start()

    zero_rows = jnp.zeros((PAD, width), jnp.float32)
    for k in range(SWEEPS):
        for c in range(COEFS):
            for x in range(1, nx + 1):
                field[k, c, x, 0:PAD] = zero_rows
                field[k, c, x, PAD + ny : 2 * PAD + ny] = zero_rows

    zero_plane = jnp.zeros((ny, width), jnp.float32)

    @pl.when(s == 0)
    def _():
        for k in range(SWEEPS):
            for c in range(COEFS):
                field[k, c, 0, PAD : PAD + ny] = zero_plane

    @pl.when(s == n_space - 1)
    def _():
        for k in range(SWEEPS):
            for c in range(COEFS):
                field[k, c, nx + 1, PAD : PAD + ny] = zero_plane

    @pl.when(e == 0)
    def _():
        for k in range(SWEEPS):
            from_low[k] = jnp.zeros(from_low.shape[1:], jnp.float32)

    @pl.when(e == n_energy - 1)
    def _():
        for k in range(SWEEPS):
            from_high[k] = jnp.zeros(from_high.shape[1:], jnp.float32)

    for load in loads[:6]:
        load.wait()

    region = regions_ref[...]
    off = jnp.zeros_like(region)
    absorb = jnp.zeros(region.shape, jnp.float32)
    emit = jnp.zeros(region.shape, jnp.float32)
    for r in range(REGIONS):
        inside = region == r
        off = jnp.where(inside, offsets_ref[r], off)
        absorb = jnp.where(inside, phonon_ref[0, r], absorb)
        emit = jnp.where(inside, phonon_ref[1, r], emit)

    def spread(*pairs):
        for source, target in pairs:
            turned = source.T
            for x in range(nx):
                target[x] = jnp.broadcast_to(turned[:, x : x + 1], (ny, width))

    spread((fields_ref[0], cell_x), (fields_ref[1], cell_y), (contacts_ref[...], cell_pin))

    for load in loads[6:]:
        load.wait()

    def solve(r, px, py, diag, inv_d, inv_t):
        first = (diag * r[0] - px * r[1] - py * r[2]) * inv_t
        return (
            first,
            (r[1] + px * first) * inv_d,
            (r[2] + py * first) * inv_d,
            r[3] * inv_d,
        )

    half = nx // 2

    def plane_at(i):
        turned, step = i % 2, i // 2
        return step + turned * (nx - 1 - 2 * step)

    def first_state(i, carry):
        x = plane_at(i)
        for y in range(0, ny, ROWS):
            rows = pl.ds(y, ROWS)
            diag = rate[x, rows] + 4.0 * diffusion
            px, py = cell_x[x, rows], cell_y[x, rows]
            inv_d = 1.0 / diag
            inv_t = 1.0 / (diag * diag + px * px + py * py)
            inv_diag[x, rows] = inv_d
            inv_det[x, rows] = inv_t
            r = [right[c, x, rows] for c in range(COEFS)]
            u = solve(r, px, py, diag, inv_d, inv_t)
            pinned = cell_pin[x, rows] == 1
            for c in range(COEFS):
                field[0, c, x + 1, pl.ds(PAD + y, ROWS)] = jnp.where(pinned, r[c], u[c])
        return carry

    lax.fori_loop(0, half, first_state, 0)
    pl.semaphore_wait(barrier, n_energy + n_space - 2)
    for step in range(1, n_energy):
        pl.semaphore_signal(
            known,
            inc=1,
            device_id=(lax.rem(e + step, n_energy), s),
            device_id_type=MESH,
        )

    unit_lane = lax.broadcasted_iota(jnp.int32, (8, width), 1)
    units = [
        [(plane_at(i), y) for i in part for y in range(0, ny, 8)]
        for part in (range(half), range(half, nx))
    ]
    inner = pl.ds(PAD, ny)

    def to_right(k):
        return pltpu.make_async_remote_copy(
            src_ref=field.at[k, :, nx, inner],
            dst_ref=field.at[k, :, 0, inner],
            send_sem=x_send.at[k, 0],
            recv_sem=x_recv.at[k, 0],
            device_id=(e, s + 1),
            device_id_type=MESH,
        )

    def to_left(k):
        return pltpu.make_async_remote_copy(
            src_ref=field.at[k, :, 1, inner],
            dst_ref=field.at[k, :, nx + 1, inner],
            send_sem=x_send.at[k, 1],
            recv_sem=x_recv.at[k, 1],
            device_id=(e, s - 1),
            device_id_type=MESH,
        )

    def to_upper(k, g):
        return pltpu.make_async_remote_copy(
            src_ref=pack_high.at[k, g],
            dst_ref=from_low.at[k, g],
            send_sem=e_send.at[k, g, 0],
            recv_sem=e_recv.at[k, g, 0],
            device_id=(e + 1, s),
            device_id_type=MESH,
        )

    def to_lower(k, g):
        return pltpu.make_async_remote_copy(
            src_ref=pack_low.at[k, g],
            dst_ref=from_high.at[k, g],
            send_sem=e_send.at[k, g, 1],
            recv_sem=e_recv.at[k, g, 1],
            device_id=(e - 1, s),
            device_id_type=MESH,
        )

    has_right, has_left = s < n_space - 1, s > 0
    has_upper, has_lower = e < n_energy - 1, e > 0

    def turn(value, by):
        by = by % width
        return pltpu.roll(value, by, 1) if by else value

    def exchange(k, g):
        if g == 0:

            @pl.when(has_right)
            def _():
                to_right(k).start()

            @pl.when(has_left)
            def _():
                to_left(k).start()

        for q in range(pack_low.shape[2]):
            low = jnp.zeros((8, width), jnp.float32)
            high = jnp.zeros((8, width), jnp.float32)
            for j, (x, y) in enumerate(units[g][q * groups : (q + 1) * groups]):
                part = field[k, 0, x + 1, pl.ds(PAD + y, 8)]
                here = (unit_lane >= HOP * j) & (unit_lane < HOP * (j + 1))
                low = jnp.where(here, turn(part, HOP * j), low)
                high = jnp.where(here, turn(part, HOP * (j + 1)), high)
            pack_low[k, g, q] = low
            pack_high[k, g, q] = high

        @pl.when(has_upper)
        def _():
            to_upper(k, g).start()

        @pl.when(has_lower)
        def _():
            to_lower(k, g).start()

    def arrive(k, g):
        @pl.when(has_lower)
        def _():
            to_upper(k, g).wait_recv()

        @pl.when(has_upper)
        def _():
            to_lower(k, g).wait_recv()

        for i, (x, y) in enumerate(units[g]):
            q, j = i // groups, i % groups
            beyond[x, pl.ds(y, 8)] = jnp.where(
                unit_lane < width // 2,
                turn(from_high[k, g, q], -HOP * j),
                turn(from_low[k, g, q], -HOP * (j + 1)),
            )

        if g == 0:

            @pl.when(has_left)
            def _():
                to_right(k).wait_recv()

            @pl.when(has_right)
            def _():
                to_left(k).wait_recv()

    exchange(0, 0)
    lax.fori_loop(half, nx, first_state, 0)
    exchange(0, 1)
    spread((off, cell_off), (absorb, cell_absorb), (emit, cell_emit))

    lane = lax.broadcasted_iota(jnp.int32, (ROWS, width), 1)
    velocity = jnp.broadcast_to(0.5 * speed_ref[...], (ROWS, width))

    def residual(k, x, y):
        rows = pl.ds(y, ROWS)
        mid = pl.ds(PAD + y, ROWS)
        f = [field[k, c, x + 1, mid] for c in range(COEFS)]
        xp = [field[k, c, x + 2, mid] for c in range(COEFS)]
        xm = [field[k, c, x, mid] for c in range(COEFS)]
        yp = [field[k, c, x + 1, pl.ds(PAD + y + 1, ROWS)] for c in range(COEFS)]
        ym = [field[k, c, x + 1, pl.ds(PAD + y - 1, ROWS)] for c in range(COEFS)]
        diag = rate[x, rows] + 4.0 * diffusion
        px, py = cell_x[x, rows], cell_y[x, rows]
        nb = [xp[c] + xm[c] + (yp[c] + ym[c]) for c in range(COEFS)]
        outside = beyond[x, rows]
        off = cell_off[x, rows]
        below = jnp.take_along_axis(
            jnp.where(lane < width - off, f[0], outside),
            jnp.where(lane < off, lane - off + width, lane - off),
            axis=1,
            mode="promise_in_bounds",
        )
        above = jnp.take_along_axis(
            jnp.where(lane < off, outside, f[0]),
            jnp.where(lane < width - off, lane + off, lane + off - width),
            axis=1,
            mode="promise_in_bounds",
        )
        scatter = cell_absorb[x, rows] * below + cell_emit[x, rows] * above
        image = [
            diag * f[0]
            + px * f[1]
            + py * f[2]
            - diffusion * nb[0]
            + velocity * (xp[1] - xm[1] + (yp[2] - ym[2]))
            - scatter,
            diag * f[1] - px * f[0] - diffusion * nb[1] + velocity * (xp[0] - xm[0]),
            diag * f[2] - py * f[0] - diffusion * nb[2] + velocity * (yp[0] - ym[0]),
            diag * f[3] - diffusion * nb[3],
        ]
        pinned = cell_pin[x, rows] == 1
        resid = [
            right[c, x, rows] - jnp.where(pinned, f[c], image[c]) for c in range(COEFS)
        ]
        return f, resid, pinned, px, py, diag

    def folded(value):
        square = value * value
        out = square[0:8]
        for i in range(8, ROWS, 8):
            out = out + square[i : i + 8]
        return out

    def sweep(k, g, start):
        last = k == SWEEPS - 1

        def plane(i, carry):
            x = plane_at(i)
            acc = list(carry)
            for y in range(0, ny, ROWS):
                f, resid, pinned, px, py, diag = residual(k, x, y)
                for c in range(COEFS):
                    acc[c] = acc[c] + folded(resid[c])
                if not last:
                    rows = pl.ds(y, ROWS)
                    u = solve(resid, px, py, diag, inv_diag[x, rows], inv_det[x, rows])
                    for c in range(COEFS):
                        field[k + 1, c, x + 1, pl.ds(PAD + y, ROWS)] = f[c] + jnp.where(
                            pinned, resid[c], u[c]
                        )
            return tuple(acc)

        return lax.fori_loop(g * half, half if g == 0 else nx, plane, start)

    partial = []
    store = pltpu.make_async_copy(
        field.at[SWEEPS - 1, :, pl.ds(1, nx), inner], state_ref, out_sem
    )
    for k in range(SWEEPS):
        if k == SWEEPS - 1:
            store.start()
        acc = tuple(jnp.zeros((8, width), jnp.float32) for _ in range(COEFS))
        for g in range(2):
            arrive(k, g)
            acc = sweep(k, g, acc)
            if k < SWEEPS - 1:
                exchange(k + 1, g)
        partial.extend(acc)

    spot = lax.broadcasted_iota(jnp.int32, (1, width), 1)
    mine = jnp.zeros((1, width), jnp.float32)
    for i, value in enumerate(partial):
        whole = jnp.sum(jnp.sum(value, axis=0, keepdims=True), axis=1, keepdims=True)
        mine = jnp.where(spot == i, whole, mine)
    sums[me] = mine
    pl.semaphore_wait(known, n_energy - 1)

    def tell(de, ds, rows):
        return pltpu.make_async_remote_copy(
            src_ref=sums.at[rows],
            dst_ref=sums.at[rows],
            send_sem=n_send,
            recv_sem=n_recv,
            device_id=(lax.rem(e + de, n_energy), lax.rem(s + ds, n_space)),
            device_id_type=MESH,
        )

    own = pl.ds(me, 1)
    for ds in sorted(range(n_space), key=lambda d: -min(d, n_space - d)):
        for de in range(n_energy):
            if (de, ds) != (0, 0):
                tell(de, ds, own).start()
    for k in range(SWEEPS):

        @pl.when(has_right)
        def _():
            to_right(k).wait_send()

        @pl.when(has_left)
        def _():
            to_left(k).wait_send()

        for g in range(2):

            @pl.when(has_upper)
            def _():
                to_upper(k, g).wait_send()

            @pl.when(has_lower)
            def _():
                to_lower(k, g).wait_send()

    store.wait()
    others = tell(0, 1, pl.ds(0, n_energy * n_space - 1))
    others.wait_recv()
    others.wait_send()
    sums_ref[...] = jnp.sum(sums[...], axis=0)


def finish(state, sums_ref, state_hbm, norms_ref, sem):
    stores = [
        pltpu.make_async_copy(state.at[c], state_hbm.at[c], sem.at[c]) for c in range(COEFS)
    ]
    for store in stores:
        store.start()
    width = sums_ref.shape[1]
    norm = jnp.broadcast_to(jnp.sqrt(sums_ref[...]), (8, width))
    for k in range(SWEEPS):
        turned = pltpu.roll(norm, width - COEFS * k, 1) if k else norm
        norms_ref[k : k + 1, :] = turned[0:1, 0:COEFS]
    for store in stores:
        store.wait()


def solution(mesh):
    n_energy, n_space = mesh.shape["energy"], mesh.shape["space"]

    def local(right_side, rate, fields, speed, regions, contacts, offsets, phonon):
        coefs, nx, ny, width = right_side.shape
        packs = -(-((nx - nx // 2) * ny // 8) // (width // HOP))
        plane = (nx, ny, width)
        vmem = pl.BlockSpec(memory_space=pltpu.VMEM)
        hbm = pl.BlockSpec(memory_space=pl.ANY)
        f32 = jnp.float32
        pack = pltpu.VMEM((SWEEPS, 2, packs, 8, width), f32)
        state, sums = pl.pallas_call(
            functools.partial(kernel, n_energy, n_space),
            out_shape=(
                pltpu.VMEM(right_side.shape, f32),
                pltpu.VMEM((1, width), f32),
            ),
            in_specs=[pl.BlockSpec(memory_space=pltpu.HBM)] * 8,
            out_specs=(vmem, vmem),
            scratch_shapes=[
                pltpu.SMEM(offsets.shape, offsets.dtype),
                pltpu.SMEM((phonon.shape[1], phonon.shape[0]), f32),
                pltpu.VMEM(fields.shape, f32),
                pltpu.VMEM((1, width), f32),
                pltpu.VMEM(regions.shape, regions.dtype),
                pltpu.VMEM(contacts.shape, contacts.dtype),
                pltpu.VMEM(right_side.shape, f32),
                pltpu.VMEM(plane, f32),
                pltpu.VMEM((SWEEPS, coefs, nx + 2, ny + 2 * PAD, width), f32),
                pltpu.VMEM(plane, f32),
                pltpu.VMEM(plane, f32),
                pltpu.VMEM(plane, jnp.int32),
                pltpu.VMEM(plane, jnp.int32),
                pltpu.VMEM(plane, f32),
                pltpu.VMEM(plane, f32),
                pltpu.VMEM(plane, f32),
                pltpu.VMEM(plane, f32),
                pack,
                pack,
                pack,
                pack,
                pltpu.VMEM(plane, f32),
                pltpu.VMEM((n_energy * n_space, 1, width), f32),
                pltpu.SemaphoreType.DMA((7 + coefs,)),
                pltpu.SemaphoreType.DMA,
                pltpu.SemaphoreType.DMA((SWEEPS, 2)),
                pltpu.SemaphoreType.DMA((SWEEPS, 2)),
                pltpu.SemaphoreType.DMA((SWEEPS, 2, 2)),
                pltpu.SemaphoreType.DMA((SWEEPS, 2, 2)),
                pltpu.SemaphoreType.DMA,
                pltpu.SemaphoreType.DMA,
                pltpu.SemaphoreType.REGULAR,
            ],
            compiler_params=pltpu.CompilerParams(
                collective_id=0, has_side_effects=True, vmem_limit_bytes=24 << 20
            ),
        )(
            *(
                pltpu.with_memory_space_constraint(value, pltpu.HBM)
                for value in (
                    offsets,
                    phonon.T,
                    right_side,
                    rate,
                    fields,
                    speed.reshape(1, width),
                    regions,
                    contacts,
                )
            )
        )
        return pl.pallas_call(
            finish,
            out_shape=(
                jax.ShapeDtypeStruct(right_side.shape, f32),
                jax.ShapeDtypeStruct((SWEEPS, coefs), f32),
            ),
            in_specs=[vmem, vmem],
            out_specs=(hbm, vmem),
            scratch_shapes=[pltpu.SemaphoreType.DMA((coefs,))],
            compiler_params=pltpu.CompilerParams(vmem_limit_bytes=8 << 20),
        )(state, sums)

    in_specs = (
        P(None, "space", None, "energy"),
        P("space", None, "energy"),
        P(None, "space", None),
        P("energy"),
        P("space", None),
        P("space", None),
        P(),
        P(),
    )
    out_specs = (P(None, "space", None, "energy"), P())
    return jax.shard_map(local, mesh=mesh, in_specs=in_specs, out_specs=out_specs, check_vma=False)
```
